32 devices in a mesh: fsdp: 8 (over y, x, core), ctx: 4 (over z).
Axes of the slice: x: 2, y: 2, z: 4, core: 2. Of those that a mesh axis runs over, the one named last changes fastest.
Arguments:
- tokens: bfloat16 [16, 4, 256, 1536], P('fsdp', 'ctx'), may hold values from -6 to 6
- block_pairs: int32 [16, 4], P('fsdp'), may hold values from 0 to 3, each once within a row
- gain_attn: bfloat16 [1536], P('fsdp'), may hold values from 0.25 to 1.75
- w_qkv: bfloat16 [1536, 3072], P('fsdp'), may hold values from -0.15625 to 0.15625
- w_out: bfloat16 [1536, 1536], P('fsdp'), may hold values from -0.625 to 0.625
- gain_ffn: bfloat16 [1536], P('fsdp'), may hold values from 0.25 to 1.75
- w_gate: bfloat16 [1536, 4096], P('fsdp'), may hold values from -0.15625 to 0.15625
- w_up: bfloat16 [1536, 4096], P('fsdp'), may hold values from -0.15625 to 0.15625
- w_down: bfloat16 [4096, 1536], P('fsdp'), may hold values from -0.09375 to 0.09375
- cotangent: bfloat16 [16, 4, 256, 1536], P('fsdp', 'ctx'), may hold values from -6 to 6
Outputs:
- output: bfloat16 [16, 4, 256, 1536], P('fsdp', 'ctx')
- grad_tokens: bfloat16 [16, 4, 256, 1536], P('fsdp', 'ctx')
- grad_gain_attn: float32 [1536], P('fsdp')
- grad_w_qkv: float32 [1536, 3072], P('fsdp')
- grad_w_out: float32 [1536, 1536], P('fsdp')
- grad_gain_ffn: float32 [1536], P('fsdp')
- grad_w_gate: float32 [1536, 4096], P('fsdp')
- grad_w_up: float32 [1536, 4096], P('fsdp')
- grad_w_down: float32 [4096, 1536], P('fsdp')
The draws below stay inside these ranges and needn't reach their ends.
Inputs may be any that keep to these rules, and one draw needn't show every extreme that they name: `block_pairs`: each row names every pair 0 to 3 once.
All inputs are finite; a program needn't handle non-finite values.
Results may differ from the reference program's by a relative error of at most 0.02.
Values may be sent and summed in bfloat16 or wider, within the bound.
No kernel may reach another device: no remote copies, remote signals or barrier semaphores. Data moves between devices by JAX's collectives and lax.ppermute only.
A program may use at most 320 MiB of HBM per device.

```python
import jax
import jax.numpy as jnp
from jax import lax

D = 1536
HEADS = 16
KV_HEADS = 8
HD = 96
FF = 4096
BLK = 128
SEQS = 16
N_CTX = 4


def steps_of(key, extent, pieces, smallest, top_value):
    level, own = 1.0, jax.random.fold_in(key, 6)
    for axis_at, shards_of in pieces:
        heights = jnp.exp(jax.random.uniform(jax.random.fold_in(own, axis_at), (shards_of,), jnp.float32, smallest / len(pieces), top_value / len(pieces)))
        level = level * jnp.repeat(heights, extent[axis_at] // shards_of).reshape([-1 if axis == axis_at else 1 for axis in range(len(extent))])
    return level


def centred(stream_key, dims, deviation, reach, split=(), kind=jnp.bfloat16):
    values = deviation * jax.random.normal(stream_key, dims, jnp.float32)
    if split:
        values = values * steps_of(stream_key, dims, split, -0.22, 0.18)
    return jnp.clip(values, -reach, reach).astype(kind)


def setup_inputs(seed: int = 0) -> dict:
    arg_keys = jax.random.split(jax.random.key(seed), 11)
    tokens = centred(arg_keys[0], (SEQS, N_CTX, 2 * BLK, D), 1.0, 6.0, ((0, 8), (1, 4)))
    block_pairs = jax.vmap(lambda own: jax.random.permutation(own, N_CTX))(jax.random.split(arg_keys[1], SEQS)).reshape((SEQS, N_CTX)).astype(jnp.int32)
    gain_attn = jnp.clip(1.0 + 0.15 * jax.random.normal(arg_keys[2], (D,), jnp.float32), 0.25, 1.75).astype(jnp.bfloat16)
    w_qkv = centred(arg_keys[3], (D, (HEADS + 2 * KV_HEADS) * HD), D ** -0.5, 0.15625, ((0, 8),))
    w_out = centred(arg_keys[4], (HEADS * HD, D), (HEADS * HD // 16) ** -0.5, 0.625, ((0, 8),))
    gain_ffn = jnp.clip(1.0 + 0.15 * jax.random.normal(arg_keys[5], (D,), jnp.float32), 0.25, 1.75).astype(jnp.bfloat16)
    w_gate = centred(arg_keys[6], (D, FF), D ** -0.5, 0.15625, ((0, 8),))
    w_up = centred(arg_keys[7], (D, FF), D ** -0.5, 0.15625, ((0, 8),))
    w_down = centred(arg_keys[8], (FF, D), FF ** -0.5, 0.09375, ((0, 8),))
    cotangent = centred(arg_keys[9], (SEQS, N_CTX, 2 * BLK, D), 1.0, 6.0, ((0, 8), (1, 4)))
    return dict(tokens=tokens, block_pairs=block_pairs, gain_attn=gain_attn, w_qkv=w_qkv, w_out=w_out, gain_ffn=gain_ffn, w_gate=w_gate, w_up=w_up, w_down=w_down, cotangent=cotangent)


EPS = 1e-05
ROPE_BASE = 100000.0

@jax.custom_vjp
def low(v):
    return lax.optimization_barrier(v.astype(jnp.bfloat16)).astype(jnp.float32)

@jax.custom_vjp
def low_back(v):
    return v

def low_keep(v):
    return (low(v), None)

def low_pass(kept, grad):
    return (grad,)

def back_keep(v):
    return (v, None)

def back_low(kept, grad):
    return (low(grad),)
low.defvjp(low_keep, low_pass)
low_back.defvjp(back_keep, back_low)

def rope_tables(positions):
    exponents = jnp.arange(HD // 2, dtype=jnp.float32) * 2.0 / HD
    inverse = 1.0 / ROPE_BASE ** exponents
    angles = positions.astype(jnp.float32)[:, None] * inverse[None, :]
    return (jnp.cos(angles), jnp.sin(angles))

def rotate(vectors, cosine, sine_table):
    half_size = vectors.shape[-1] // 2
    front_half = vectors[..., :half_size]
    back_half = vectors[..., half_size:]
    cos_wide = cosine[:, None, :]
    sin_wide = sine_table[:, None, :]
    return jnp.concatenate([front_half * cos_wide - back_half * sin_wide, back_half * cos_wide + front_half * sin_wide], axis=-1)

def block_positions(pair_ids, ctx_count, block_rows):
    offsets = jnp.arange(2 * block_rows, dtype=jnp.int32)
    mirror = 2 * ctx_count - 1 - pair_ids[..., None]
    block_ids = jnp.where(offsets < block_rows, pair_ids[..., None], mirror)
    return block_ids * block_rows + offsets % block_rows

def sequence_block(gain_attn, w_qkv, w_out, gain_ffn, w_gate, w_up, w_down, seq_tokens, pair_ids):
    highest = lax.Precision.HIGHEST
    query_width = HEADS * HD
    kv_width = KV_HEADS * HD
    group_size = HEADS // KV_HEADS
    token_rows = seq_tokens.reshape(-1, D)
    positions = block_positions(pair_ids, N_CTX, BLK).reshape(-1)
    cosine, sine_table = rope_tables(positions)
    scale_one = lax.rsqrt(lax.optimization_barrier(jnp.mean(token_rows * token_rows, axis=-1, keepdims=True)) + EPS)
    normed_one = low(token_rows * scale_one * gain_attn)
    projected = jnp.dot(normed_one, w_qkv, precision=highest)
    queries = low_back(projected[:, :query_width])
    keys_rot = low_back(projected[:, query_width:query_width + kv_width])
    values = low_back(projected[:, query_width + kv_width:])
    queries = low(rotate(queries.reshape(-1, HEADS, HD), cosine, sine_table))
    keys_rot = low(rotate(keys_rot.reshape(-1, KV_HEADS, HD), cosine, sine_table))
    values = low(values.reshape(-1, KV_HEADS, HD))
    grouped = queries.reshape(-1, KV_HEADS, group_size, HD)
    scores = low_back(jnp.einsum('qgrd,kgd->grqk', grouped, keys_rot, precision=highest) * HD ** (-0.5))
    allowed = positions[None, :] <= positions[:, None]
    scores = jnp.where(allowed, scores, -1e+30)
    attn_weights = low(jax.nn.softmax(scores, axis=-1))
    attended = jnp.einsum('grqk,kgd->qgrd', attn_weights, values, precision=highest).reshape(-1, query_width)
    attended = low(low_back(attended))
    middle = token_rows + low_back(jnp.dot(attended, w_out, precision=highest))
    scale_two = lax.rsqrt(lax.optimization_barrier(jnp.mean(middle * middle, axis=-1, keepdims=True)) + EPS)
    normed_two = low(middle * scale_two * gain_ffn)
    gate_proj = low_back(jnp.dot(normed_two, w_gate, precision=highest))
    up_proj = low_back(jnp.dot(normed_two, w_up, precision=highest))
    hidden = low(jax.nn.silu(gate_proj) * up_proj)
    result = middle + low_back(jnp.dot(hidden, w_down, precision=highest))
    return result.reshape(seq_tokens.shape)

def reference(tokens, block_pairs, gain_attn, w_qkv, w_out, gain_ffn, w_gate, w_up, w_down, cotangent):
    weights = [array.astype(jnp.float32) for array in (gain_attn, w_qkv, w_out, gain_ffn, w_gate, w_up, w_down)]
    inputs = tokens.astype(jnp.float32)

    def forward(inputs, gain_one, qkv_full, out_full, gain_two, gate_full, up_full, down_full):
        block_fn = jax.checkpoint(sequence_block)

        def single_sequence(carry_args):
            return block_fn(gain_one, qkv_full, out_full, gain_two, gate_full, up_full, down_full, carry_args[0], carry_args[1])
        return lax.map(single_sequence, (inputs, block_pairs))
    result, pullback = jax.vjp(forward, inputs, *weights)
    gradients = pullback(cotangent.astype(jnp.float32))
    return (result.astype(jnp.bfloat16), gradients[0].astype(jnp.bfloat16), gradients[1], gradients[2], gradients[3], gradients[4], gradients[5], gradients[6], gradients[7])
```

```python
import functools
import jax
import jax.numpy as jnp
from jax import lax
from jax.experimental import pallas as pl
from jax.experimental.pallas import tpu as pltpu
from jax.sharding import PartitionSpec as P

D = 1536
HEADS = 16
KV_HEADS = 8
HD = 96
GROUPS = 2
KV_G = KV_HEADS // GROUPS
QW = HEADS * HD // GROUPS
KW = KV_HEADS * HD // GROUPS
MASKED = -1e30
SCALE = HD ** -0.5
NT = (((1,), (1,)), ((), ()))
TN = (((0,), (0,)), ((), ()))


def dot(a, b, dims=(((1,), (0,)), ((), ()))):
    return lax.dot_general(a, b, dims, preferred_element_type=jnp.float32)


def fill_bias(ids_ref, bias_ref, slots, blk):
    own = ids_ref[slots]
    key = lax.broadcasted_iota(jnp.int32, (blk, 2 * blk), 0)
    query = lax.broadcasted_iota(jnp.int32, (blk, 2 * blk), 1)
    query = jnp.where(query >= blk, query - blk, query)
    for slot in range(slots):
        pair = ids_ref[slot]
        low = key + (pair - own) * blk <= query
        high = key + (own - pair) * blk <= query
        bias_ref[0, slot * blk : (slot + 1) * blk, :] = jnp.where(low, 0.0, MASKED)
        bias_ref[1, slot * blk : (slot + 1) * blk, :] = jnp.where(high, 0.0, MASKED)


def halves(ref, slots, blk, head):
    cols = slice(head * HD, (head + 1) * HD)
    low = ref[:, :blk, cols].reshape(slots * blk, HD)
    high = ref[:, blk:, cols].reshape(slots * blk, HD)
    return low, high


def pair_rows(ref, blk, head, high):
    rows = slice(blk, 2 * blk) if high else slice(0, blk)
    first = ref[rows, 2 * head * HD : (2 * head + 1) * HD]
    second = ref[rows, (2 * head + 1) * HD : (2 * head + 2) * HD]
    return jnp.concatenate([first, second], axis=0)


def attend_kernel(slots, blk, ids_ref, q_ref, k_ref, v_ref, out_ref, lse_ref, bias_ref):
    @pl.when(pl.program_id(0) == 0)
    def _():
        fill_bias(ids_ref, bias_ref, slots, blk)

    lows, highs = [], []
    for head in range(KV_G):
        kl, kh = halves(k_ref, slots, blk, head)
        vl, vh = halves(v_ref, slots, blk, head)
        ql = pair_rows(q_ref, blk, head, False)
        qh = pair_rows(q_ref, blk, head, True)
        sll = dot(kl, ql, NT) * SCALE + bias_ref[0]
        top = jnp.max(sll, axis=0, keepdims=True)
        p = jnp.exp(sll - top)
        total = jnp.sum(p, axis=0, keepdims=True)
        o = dot(vl, p.astype(jnp.bfloat16), TN) / total
        lse_ref[0, 2 * head : 2 * head + 1, :] = top + jnp.log(total)
        o = o.T
        lows += [o[:blk], o[blk:]]
        shl = dot(kl, qh, NT) * SCALE
        shh = dot(kh, qh, NT) * SCALE + bias_ref[1]
        top = jnp.maximum(
            jnp.max(shl, axis=0, keepdims=True), jnp.max(shh, axis=0, keepdims=True)
        )
        pl_ = jnp.exp(shl - top)
        ph = jnp.exp(shh - top)
        total = jnp.sum(pl_, axis=0, keepdims=True) + jnp.sum(ph, axis=0, keepdims=True)
        o = dot(vl, pl_.astype(jnp.bfloat16), TN) + dot(vh, ph.astype(jnp.bfloat16), TN)
        o = o / total
        lse_ref[0, 2 * head + 1 : 2 * head + 2, :] = top + jnp.log(total)
        o = o.T
        highs += [o[:blk], o[blk:]]
    out_ref[:blk, :] = jnp.concatenate(lows, axis=1).astype(jnp.bfloat16)
    out_ref[blk:, :] = jnp.concatenate(highs, axis=1).astype(jnp.bfloat16)


def attend(ids, q, kv_all, seq=0):
    slots, rows, _ = kv_all.shape
    blk = rows // 2
    pairs = slots * rows * rows * HEADS * 3 // 4
    return pl.pallas_call(
        functools.partial(attend_kernel, slots, blk),
        grid_spec=pltpu.PrefetchScalarGridSpec(
            num_scalar_prefetch=1,
            grid=(GROUPS,),
            in_specs=[
                pl.BlockSpec((rows, QW), lambda g, ids: (seq, g)),
                pl.BlockSpec((slots, rows, KW), lambda g, ids: (0, 0, g)),
                pl.BlockSpec((slots, rows, KW), lambda g, ids: (0, 0, GROUPS + g)),
            ],
            out_specs=[
                pl.BlockSpec((rows, QW), lambda g, ids: (0, g)),
                pl.BlockSpec((1, 2 * KV_G, 2 * blk), lambda g, ids: (g, 0, 0)),
            ],
            scratch_shapes=[pltpu.VMEM((2, slots * blk, 2 * blk), jnp.float32)],
        ),
        out_shape=[
            jax.ShapeDtypeStruct((rows, HEADS * HD), jnp.bfloat16),
            jax.ShapeDtypeStruct((GROUPS, 2 * KV_G, 2 * blk), jnp.float32),
        ],
        cost_estimate=pl.CostEstimate(
            flops=4 * pairs * HD, transcendentals=pairs, bytes_accessed=8 << 20
        ),
        name="attend",
    )(ids, q, kv_all, kv_all)


def turn(x, cosine, sine):
    width = x.shape[-1]
    lane = lax.broadcasted_iota(jnp.int32, x.shape, 1) % HD
    other = jnp.where(
        lane < HD // 2, pltpu.roll(x, width - HD // 2, 1), pltpu.roll(x, HD // 2, 1)
    )
    return x * cosine + other * sine


def attend_back_kernel(
    slots, blk, ids_ref, q_ref, k_ref, v_ref, do_ref, lse_ref, cos_ref, sin_ref,
    dq_ref, dkv_ref, bias_ref,
):
    @pl.when(pl.program_id(0) == 0)
    def _():
        fill_bias(ids_ref, bias_ref, slots, blk)

    bf16 = jnp.bfloat16
    lows, highs, dks, dvs = [], [], [], []
    for head in range(KV_G):
        kl, kh = halves(k_ref, slots, blk, head)
        vl, vh = halves(v_ref, slots, blk, head)
        ql = pair_rows(q_ref, blk, head, False)
        qh = pair_rows(q_ref, blk, head, True)
        dol = pair_rows(do_ref, blk, head, False)
        doh = pair_rows(do_ref, blk, head, True)
        lse = lse_ref[0, 2 * head : 2 * head + 1, :]
        p = jnp.exp(dot(kl, ql, NT) * SCALE + bias_ref[0] - lse)
        dp = dot(vl, dol, NT)
        total = jnp.sum(p * dp, axis=0, keepdims=True)
        ds = (p * (dp - total)).astype(bf16)
        dq = dot(kl, ds, TN).T
        lows += [dq[:blk], dq[blk:]]
        dkl = dot(ds, ql)
        dvl = dot(p.astype(bf16), dol)
        lse = lse_ref[0, 2 * head + 1 : 2 * head + 2, :]
        pa = jnp.exp(dot(kl, qh, NT) * SCALE - lse)
        pb = jnp.exp(dot(kh, qh, NT) * SCALE + bias_ref[1] - lse)
        dpa = dot(vl, doh, NT)
        dpb = dot(vh, doh, NT)
        total = jnp.sum(pa * dpa, axis=0, keepdims=True) + jnp.sum(pb * dpb, axis=0, keepdims=True)
        dsa = (pa * (dpa - total)).astype(bf16)
        dsb = (pb * (dpb - total)).astype(bf16)
        dq = (dot(kl, dsa, TN) + dot(kh, dsb, TN)).T
        highs += [dq[:blk], dq[blk:]]
        dkl = (dkl + dot(dsa, qh)) * SCALE
        dkh = dot(dsb, qh) * SCALE
        dvl = dvl + dot(pa.astype(bf16), doh)
        dvh = dot(pb.astype(bf16), doh)
        join = lambda a, b: jnp.concatenate(
            [a.reshape(slots, blk, HD), b.reshape(slots, blk, HD)], axis=1
        )
        dks.append(join(dkl, dkh))
        dvs.append(join(dvl, dvh))
    dq = jnp.concatenate(
        [jnp.concatenate(lows, axis=1), jnp.concatenate(highs, axis=1)], axis=0
    )
    dq_ref[...] = turn(dq * SCALE, cos_ref[...], -sin_ref[...]).astype(bf16)
    dkv_ref[...] = jnp.concatenate(dks + dvs, axis=2).astype(bf16)


def attend_back(ids, q, kv_all, grad_att, lse, cosine, sine, seq=0):
    slots, rows, _ = kv_all.shape
    blk = rows // 2
    pairs = slots * rows * rows * HEADS * 3 // 4
    return pl.pallas_call(
        functools.partial(attend_back_kernel, slots, blk),
        grid_spec=pltpu.PrefetchScalarGridSpec(
            num_scalar_prefetch=1,
            grid=(GROUPS,),
            in_specs=[
                pl.BlockSpec((rows, QW), lambda g, ids: (seq, g)),
                pl.BlockSpec((slots, rows, KW), lambda g, ids: (0, 0, g)),
                pl.BlockSpec((slots, rows, KW), lambda g, ids: (0, 0, GROUPS + g)),
                pl.BlockSpec((rows, QW), lambda g, ids: (seq, g)),
                pl.BlockSpec((1, 2 * KV_G, 2 * blk), lambda g, ids: (g, 0, 0)),
                pl.BlockSpec((rows, QW), lambda g, ids: (seq, 0)),
                pl.BlockSpec((rows, QW), lambda g, ids: (seq, 0)),
            ],
            out_specs=[
                pl.BlockSpec((rows, QW), lambda g, ids: (0, g)),
                pl.BlockSpec((slots, rows, 2 * KW), lambda g, ids: (0, 0, g)),
            ],
            scratch_shapes=[pltpu.VMEM((2, slots * blk, 2 * blk), jnp.float32)],
        ),
        out_shape=[
            jax.ShapeDtypeStruct((rows, HEADS * HD), jnp.bfloat16),
            jax.ShapeDtypeStruct((slots, rows, 2 * KV_HEADS * HD), jnp.bfloat16),
        ],
        cost_estimate=pl.CostEstimate(
            flops=10 * pairs * HD, transcendentals=pairs, bytes_accessed=12 << 20
        ),
        name="attend_back",
    )(ids, q, kv_all, kv_all, grad_att, lse, cosine, sine)


EPS = 1e-05
ROPE_BASE = 100000.0


def rope_tables(positions):
    lane = jnp.arange(QW, dtype=jnp.int32) % HD
    exponents = (lane % (HD // 2)).astype(jnp.float32) * 2.0 / HD
    inverse = 1.0 / ROPE_BASE**exponents
    angles = positions.astype(jnp.float32)[:, None] * inverse[None, :]
    sign = jnp.where(lane < HD // 2, -1.0, 1.0)
    return jnp.cos(angles), jnp.sin(angles) * sign[None, :]


def block_positions(pair_ids, ctx_count, block_rows):
    offsets = jnp.arange(2 * block_rows, dtype=jnp.int32)
    mirror = 2 * ctx_count - 1 - pair_ids[..., None]
    block_ids = jnp.where(offsets < block_rows, pair_ids[..., None], mirror)
    return block_ids * block_rows + offsets % block_rows


def project_kernel(turned, order_ref, x_ref, own_ref, other_ref, cos_ref, sin_ref, out_ref, full_ref):
    chips = order_ref.shape[0] // 2
    shard = own_ref.shape[0] // chips
    for side, ref in enumerate((own_ref, other_ref)):
        for k in range(chips):
            start = pl.multiple_of(order_ref[side * chips + k] * shard, 16)
            full_ref[pl.ds(start, shard), :] = ref[k * shard : (k + 1) * shard, :]
    y = dot(x_ref[...], full_ref[...])

    @pl.when(pl.program_id(0) < turned)
    def _():
        out_ref[...] = turn(y, cos_ref[...], sin_ref[...]).astype(jnp.bfloat16)

    @pl.when(pl.program_id(0) >= turned)
    def _():
        out_ref[...] = y.astype(jnp.bfloat16)


def project(order, x, own, other, cosine, sine, turned):
    rows, depth = x.shape
    half, width = own.shape
    return pl.pallas_call(
        functools.partial(project_kernel, turned),
        grid_spec=pltpu.PrefetchScalarGridSpec(
            num_scalar_prefetch=1,
            grid=(width // QW,),
            in_specs=[
                pl.BlockSpec((rows, depth), lambda n, order: (0, 0)),
                pl.BlockSpec((half, QW), lambda n, order: (0, n)),
                pl.BlockSpec((half, QW), lambda n, order: (0, n)),
                pl.BlockSpec((rows, QW), lambda n, order: (0, 0)),
                pl.BlockSpec((rows, QW), lambda n, order: (0, 0)),
            ],
            out_specs=[
                pl.BlockSpec((rows, QW), lambda n, order: (0, n)),
                pl.BlockSpec((depth, QW), lambda n, order: (0, n)),
            ],
        ),
        out_shape=[
            jax.ShapeDtypeStruct((rows, width), jnp.bfloat16),
            jax.ShapeDtypeStruct((depth, width), jnp.bfloat16),
        ],
        cost_estimate=pl.CostEstimate(
            flops=2 * rows * depth * width, transcendentals=0, bytes_accessed=6 * depth * width
        ),
        name="project",
    )(order, x, own, other, cosine, sine)


def unturn_kernel(raw_ref, cos_ref, sin_ref, out_ref):
    raw = raw_ref[...].astype(jnp.float32)
    keys = jnp.concatenate([raw[:, 2 * g * KW : (2 * g + 1) * KW] for g in range(GROUPS)], axis=1)
    out_ref[:, :QW] = turn(keys, cos_ref[...], -sin_ref[...]).astype(jnp.bfloat16)
    for g in range(GROUPS):
        out_ref[:, QW + g * KW : QW + (g + 1) * KW] = raw_ref[
            :, (2 * g + 1) * KW : (2 * g + 2) * KW
        ]


def unturn(raw, cosine, sine):
    return pl.pallas_call(
        unturn_kernel,
        out_shape=jax.ShapeDtypeStruct(raw.shape, jnp.bfloat16),
        name="unturn",
    )(raw, cosine, sine)


def swap(x, mask):
    count = lax.axis_size("fsdp")
    return lax.ppermute(x, "fsdp", [(i, i ^ mask) for i in range(count)])


def gather_chips(x, masks):
    have = {0: x}
    for mask in masks:
        for k in list(have):
            have[k | (mask >> 1)] = swap(have[k], mask)
    return [have[k] for k in sorted(have)]


def pick(received, keys):
    wanted = []
    for known, array in received:
        rows = array.shape[0] // len(known)
        parts = [array[known.index(k) * rows : (known.index(k) + 1) * rows] for k in keys]
        wanted.append(parts[0] if len(parts) == 1 else jnp.concatenate(parts, axis=0))
    return wanted


def scatter_chips(columns, right, masks, received):
    def value(keys):
        total = jnp.einsum(
            "rd,rf->df", columns(keys), right, preferred_element_type=jnp.float32
        )
        for part in pick(received, keys):
            total = total + part.astype(jnp.float32)
        return total.astype(jnp.bfloat16)

    received = list(received)
    kept = list(range(lax.axis_size("fsdp") // 2))
    for mask in masks:
        bit = mask >> 1
        away = [k for k in kept if k & bit]
        kept = [k for k in kept if not k & bit]
        received.append((kept, swap(value(away), mask)))
    return value([0])


def line_sum(x):
    count = lax.axis_size("ctx")
    place = lax.axis_index("ctx")
    half = count // 2

    def plus(a, b):
        return (a.astype(jnp.float32) + b.astype(jnp.float32)).astype(jnp.bfloat16)

    for i in range(half - 1):
        x = plus(x, lax.ppermute(x, "ctx", [(i, i + 1), (count - 1 - i, count - 2 - i)]))
    x = plus(x, lax.ppermute(x, "ctx", [(half - 1, half), (half, half - 1)]))
    for i in range(half - 2, -1, -1):
        back = lax.ppermute(x, "ctx", [(i + 1, i), (count - 2 - i, count - 1 - i)])
        x = jnp.where((place == i) | (place == count - 1 - i), back, x)
    return x


def norm_back(grad_normed, token_rows, scale_rows, gain_vector):
    scaled = token_rows * scale_rows
    weighted = grad_normed * gain_vector
    grad_gain = jnp.sum(grad_normed * scaled, axis=0)
    grad_rows = scale_rows * (
        weighted - scaled * jnp.mean(weighted * scaled, axis=-1, keepdims=True)
    )
    return (grad_rows, grad_gain)


def per_device(
    tokens, block_pairs, gain_attn, w_qkv, w_out, gain_ffn, w_gate, w_up, w_down, cotangent
):
    f32, bf16 = jnp.float32, jnp.bfloat16
    seq_count = tokens.shape[0]
    rows_pair = tokens.shape[2]
    rows = seq_count * rows_pair
    ctx_count = lax.axis_size("ctx")
    fsdp_count = lax.axis_size("fsdp")
    chips = fsdp_count // 2
    place = lax.axis_index("fsdp")
    core, chip = place % 2, place // 2
    ctx_place = lax.axis_index("ctx")
    query_width = HEADS * HD
    kv_width = KV_HEADS * HD
    shard = w_qkv.shape[0]
    ff_width = w_gate.shape[1]
    ff_chunk = ff_width // fsdp_count
    masks = [1 << (i + 1) for i in range(chips.bit_length() - 1)]
    first, second = masks, masks[::-1]
    parities = [[2 * k + c for k in range(chips)] for c in range(2)]

    picked = jnp.arange(ctx_count, dtype=jnp.int32)[None, :] == ctx_place
    own_pairs = jnp.sum(jnp.where(picked, block_pairs, 0), axis=1, keepdims=True)
    query_pos = block_positions(own_pairs, ctx_count, rows_pair // 2).reshape(seq_count, rows_pair)
    ids = jnp.concatenate([block_pairs, own_pairs], axis=1)
    cosine, sine = rope_tables(query_pos.reshape(-1))
    chip_order = jnp.arange(chips, dtype=jnp.int32) ^ chip
    order = jnp.concatenate([2 * chip_order + core, 2 * chip_order + 1 - core])

    def both(shards, masks_of):
        own = jnp.concatenate(
            [jnp.concatenate(gather_chips(w, m), axis=0) for w, m in zip(shards, masks_of)], axis=1
        ) if len(shards) == 1 else [
            jnp.concatenate(gather_chips(w, m), axis=0) for w, m in zip(shards, masks_of)
        ]
        own = own if len(shards) == 1 else jnp.concatenate(own, axis=1)
        return own, swap(own, 1)

    kv_own, kv_other = both(
        [w_qkv[:, query_width : query_width + kv_width], w_qkv[:, query_width + kv_width :]],
        [first, second],
    )
    q_own, q_other = both(
        [w_qkv[:, : query_width // 2], w_qkv[:, query_width // 2 : query_width]], [first, second]
    )
    gain_one = lax.all_gather(gain_attn, "fsdp", axis=0, tiled=True).astype(f32)
    gain_two = lax.all_gather(gain_ffn, "fsdp", axis=0, tiled=True).astype(f32)

    def wide(w):
        cut = w.reshape(shard, chips, 2, ff_chunk)
        mine = jnp.where(core == 0, cut[:, :, 0], cut[:, :, 1]).reshape(shard, -1)
        theirs = swap(jnp.where(core == 0, cut[:, :, 1], cut[:, :, 0]).reshape(shard, -1), 1)
        return jnp.concatenate(
            [jnp.where(core == 0, mine, theirs), jnp.where(core == 0, theirs, mine)], axis=0
        )

    gate_full = jnp.concatenate(gather_chips(wide(w_gate), first), axis=0)
    up_full = jnp.concatenate(gather_chips(wide(w_up), second), axis=0)
    out_full = lax.all_gather(w_out, "fsdp", axis=0, tiled=True)
    down_half = lax.all_gather(w_down, "fsdp", axis=0, tiled=True, axis_index_groups=parities)

    grad_result = cotangent.reshape(rows, D)
    grad_chip = jnp.concatenate([grad_result, swap(grad_result, 1)], axis=0)

    token_rows = tokens.reshape(rows, D).astype(f32)
    scale_one = lax.rsqrt(jnp.mean(token_rows * token_rows, axis=-1, keepdims=True) + EPS)
    normed_one = (token_rows * scale_one * gain_one).astype(bf16)
    kv, kv_full = project(order, normed_one, kv_own, kv_other, cosine, sine, 1)
    kv_all = [
        lax.all_gather(kv[s * rows_pair : (s + 1) * rows_pair], "ctx", axis=0, tiled=False)
        for s in range(seq_count)
    ]
    queries, q_full = project(order, normed_one, q_own, q_other, cosine, sine, 2)
    attended, log_total = zip(
        *[attend(ids[s], queries, kv_all[s], s) for s in range(seq_count)]
    )
    attended = jnp.concatenate(attended, axis=0)
    middle = token_rows + jnp.dot(attended, out_full, preferred_element_type=f32)
    scale_two = lax.rsqrt(jnp.mean(middle * middle, axis=-1, keepdims=True) + EPS)
    normed_two = (middle * scale_two * gain_two).astype(bf16)

    def relative(x):
        width = D // chips
        return jnp.concatenate(
            [lax.dynamic_slice_in_dim(x, (chip ^ k) * width, width, 1) for k in range(chips)],
            axis=1,
        )

    own_two = relative(normed_two)
    chip_two = jnp.concatenate([own_two, swap(own_two, 1)], axis=0)
    gate_proj = jnp.dot(chip_two, gate_full, preferred_element_type=f32)
    up_proj = jnp.dot(chip_two, up_full, preferred_element_type=f32)
    hidden = (jax.nn.silu(gate_proj) * up_proj).astype(bf16)
    result_theirs = jnp.dot(hidden[rows:], down_half, preferred_element_type=f32)
    result = (
        middle
        + jnp.dot(hidden[:rows], down_half, preferred_element_type=f32)
        + swap(result_theirs, 1)
    )
    output = result.astype(bf16).reshape(tokens.shape)

    grad_down = jnp.einsum("rf,rd->fd", hidden, grad_chip, preferred_element_type=f32)
    grad_down = lax.psum_scatter(
        grad_down.astype(bf16), "fsdp", scatter_dimension=0, tiled=True, axis_index_groups=parities
    )
    grad_hidden = jnp.einsum("rd,fd->rf", grad_chip, down_half, preferred_element_type=f32)
    sigmoid_gate = jax.nn.sigmoid(gate_proj)
    grad_gate_in = (
        grad_hidden * up_proj * sigmoid_gate * (1.0 + gate_proj * (1.0 - sigmoid_gate))
    ).astype(bf16)
    grad_up_in = (grad_hidden * gate_proj * sigmoid_gate).astype(bf16)

    def back_two(part):
        return jnp.einsum(
            "rf,df->rd", grad_gate_in[part], gate_full, preferred_element_type=f32
        ) + jnp.einsum("rf,df->rd", grad_up_in[part], up_full, preferred_element_type=f32)

    grad_normed_two = back_two(slice(0, rows)) + swap(back_two(slice(rows, None)), 1)
    grad_normed_two = relative(grad_normed_two)
    grad_rows_two, grad_gain_two = norm_back(grad_normed_two, middle, scale_two, gain_two)
    grad_middle = grad_result.astype(f32) + grad_rows_two
    grad_branch = grad_middle.astype(bf16)

    def chip_columns(keys):
        width = D // chips
        return jnp.concatenate([chip_two[:, k * width : (k + 1) * width] for k in keys], axis=1)

    grad_gate = scatter_chips(chip_columns, grad_gate_in, first, [])
    grad_up = scatter_chips(chip_columns, grad_up_in, second, [])
    grad_out = jnp.einsum("rq,rd->qd", attended, grad_branch, preferred_element_type=f32)
    grad_out = lax.psum_scatter(grad_out.astype(bf16), "fsdp", scatter_dimension=0, tiled=True)
    grad_attended = jnp.einsum(
        "rd,qd->rq", grad_branch, out_full, preferred_element_type=f32
    ).astype(bf16)

    pieces = [
        attend_back(ids[s], queries, kv_all[s], grad_attended, log_total[s], cosine, sine, s)
        for s in range(seq_count)
    ]
    grad_queries = jnp.concatenate([piece[0] for piece in pieces], axis=0)
    grad_kv = jnp.concatenate(
        [
            unturn(
                lax.psum_scatter(pieces[s][1], "ctx", scatter_dimension=0, tiled=False),
                cosine[s * rows_pair : (s + 1) * rows_pair],
                sine[s * rows_pair : (s + 1) * rows_pair],
            )
            for s in range(seq_count)
        ],
        axis=0,
    )

    everyone = list(range(chips))

    def one_columns(side):
        chunks = {
            k: lax.dynamic_slice_in_dim(normed_one, order[side * chips + k] * shard, shard, 1)
            for k in everyone
        }
        return lambda keys: jnp.concatenate([chunks[k] for k in keys], axis=1)

    mine, theirs = one_columns(0), one_columns(1)

    def scatter_all(right):
        cross = jnp.einsum(
            "rd,rf->df", theirs(everyone), right, preferred_element_type=f32
        ).astype(bf16)
        cross = swap(cross, 1)
        half = right.shape[1] // 2
        return jnp.concatenate(
            [
                scatter_chips(mine, right[:, :half], first, [(everyone, cross[:, :half])]),
                scatter_chips(mine, right[:, half:], second, [(everyone, cross[:, half:])]),
            ],
            axis=1,
        )

    grad_q = scatter_all(grad_queries)
    grad_kv_w = scatter_all(grad_kv)
    grad_normed_one = jnp.einsum(
        "rc,dc->rd", grad_queries, q_full, preferred_element_type=f32
    ) + jnp.einsum("rc,dc->rd", grad_kv, kv_full, preferred_element_type=f32)
    grad_rows_one, grad_gain_one = norm_back(grad_normed_one, token_rows, scale_one, gain_one)
    grad_tokens = (grad_middle + grad_rows_one).astype(bf16).reshape(tokens.shape)

    def unwide(g):
        g = g.reshape(2, shard, chips, 1, ff_chunk)
        keep = jnp.where(core == 0, g[0], g[1])
        other = swap(jnp.where(core == 0, g[1], g[0]), 1)
        low = jnp.where(core == 0, keep, other)
        high = jnp.where(core == 0, other, keep)
        return jnp.concatenate([low, high], axis=2).reshape(shard, ff_width)

    gains = lax.psum(jnp.stack([grad_gain_one, grad_gain_two]), ("fsdp", "ctx"))
    gains = lax.dynamic_slice_in_dim(gains, place * shard, shard, 1)
    grad_qkv = jnp.concatenate([line_sum(grad_q), line_sum(grad_kv_w)], axis=1)
    return (
        output,
        grad_tokens,
        gains[0],
        grad_qkv.astype(f32),
        line_sum(grad_out).astype(f32),
        gains[1],
        unwide(line_sum(grad_gate)).astype(f32),
        unwide(line_sum(grad_up)).astype(f32),
        line_sum(grad_down).astype(f32),
    )


def solution(mesh):
    block = P("fsdp", "ctx", None, None)
    row, vector = P("fsdp", None), P("fsdp")
    return jax.shard_map(
        per_device,
        mesh=mesh,
        in_specs=(block, row, vector, row, row, vector, row, row, row, block),
        out_specs=(block, block, vector, row, row, vector, row, row, row),
        check_vma=False,
    )
```
